512 devices in a mesh: row: 32 (over z, core), col: 16 (over y, x).
Axes of the slice: x: 4, y: 4, z: 16, core: 2. Of those that a mesh axis runs over, the one named last changes fastest.
Arguments:
- matrix: float32 [4, 32, 128, 8, 16, 128], P(None, 'row', None, None, 'col'), as said below
Outputs:
- swept: float32 [4, 32, 128, 8, 16, 128], P(None, 'row', None, None, 'col')
Inputs may be any that keep to these rules, and one draw needn't show every extreme that they name: `matrix`: every diagonal entry is at least sqrt(16384) - 6 and every off-diagonal entry has magnitude at most 6.
All inputs are finite; a program needn't handle non-finite values.
Results may differ from the reference program's by a relative error of at most 0.0001.
Values sent between devices are 32-bit elements; how exact they have to be, the bound alone decides.
No kernel may reach another device: no remote copies, remote signals or barrier semaphores. Data moves between devices by JAX's collectives and lax.ppermute only.
A program may use at most 64 MiB of HBM per device.

```python
import math
import jax
import jax.numpy as jnp
from jax import lax

ORDER = 16384
TILE = 128
PIVOTS = 3
RTD = 4
CTD = 8
N_ROW = 32
N_COL = 16


def draw_matrix(key, part):
    first, second = jax.random.split(jax.random.fold_in(key, 11), 2)
    offdiag = jnp.clip(jax.random.normal(first, (ORDER, ORDER), jnp.float32), -6.0, 6.0)
    heavy = math.sqrt(ORDER) * jax.random.uniform(second, (ORDER,), jnp.float32, 1.0, 2.0)
    indices = jnp.arange(ORDER)
    full = offdiag.at[indices, indices].add(heavy)
    return full.reshape(RTD, N_ROW, TILE, CTD, N_COL, TILE)


def setup_inputs(seed: int = 0) -> dict:
    arg_keys = jax.random.split(jax.random.key(seed), 2)
    return {
        "matrix": draw_matrix(jax.random.fold_in(arg_keys[1], 71), 0),
    }


def newton_inverse(block):
    inv_diag = 1.0 / jnp.diagonal(block)
    return 2.0 * jnp.diag(inv_diag) - inv_diag[:, None] * block * inv_diag[None, :]


def reference(matrix):
    whole = matrix.reshape(ORDER, ORDER)
    for pivot in range(PIVOTS):
        lower = pivot * TILE
        block = whole[lower:lower + TILE, lower:lower + TILE]
        inverse = newton_inverse(block)
        pivot_rows = jnp.dot(inverse, whole[lower:lower + TILE, :], precision=lax.Precision.HIGHEST)
        pivot_rows = pivot_rows.at[:, lower:lower + TILE].set(inverse)
        col_panel = whole[:, lower:lower + TILE]
        zeroed = whole.at[:, lower:lower + TILE].set(jnp.float32(0.0))
        whole = zeroed - jnp.dot(col_panel, pivot_rows, precision=lax.Precision.HIGHEST)
        whole = whole.at[lower:lower + TILE, :].set(pivot_rows)
    return whole.reshape(matrix.shape)
```

```python
import jax
import jax.numpy as jnp
from jax import lax
from jax.sharding import PartitionSpec as P

PIVOTS = 3
HI = lax.Precision.HIGHEST


def newton_inverse(block):
    inv_diag = 1.0 / jnp.diagonal(block)
    return 2.0 * jnp.diag(inv_diag) - inv_diag[:, None] * block * inv_diag[None, :]


def tree_stages(n_z):
    dist = n_z // 2
    while dist:
        yield dist
        dist //= 2


def tree_step(buf, root, dist, row, n_z):
    pairs = []
    for s in range(0, n_z, 2 * dist):
        pairs.append((2 * ((root + s) % n_z), 2 * ((root + s + dist) % n_z)))
        pairs.append((2 * ((root + s) % n_z) + 1, 2 * ((root + s - dist) % n_z) + 1))
    recv = lax.ppermute(buf, "row", pairs)
    z = (row // 2 - root + n_z) % n_z
    return jnp.where(z % (2 * dist) == dist, recv, buf)


def gather_cols(piece, n_col):
    return lax.all_to_all(
        jnp.broadcast_to(piece[None], (n_col, *piece.shape)), "col", 0, 0, tiled=True
    )


def local(matrix):
    n_row = lax.axis_size("row")
    n_col = lax.axis_size("col")
    n_z = n_row // 2
    row = lax.axis_index("row")
    col = lax.axis_index("col")
    core = row % 2
    rt, _, t, ct, _, _ = matrix.shape
    a = matrix.reshape(rt, t, ct, t)
    sub = t // n_col
    cp = a[:, :, 0, :].reshape(rt, n_col, sub, t).transpose(1, 0, 2, 3)
    cs = lax.all_to_all(cp, "col", 0, 0, tiled=True)[:PIVOTS]
    half = t // 2
    keep = lax.dynamic_slice_in_dim(a[0], core * half, half, 0)
    give = lax.dynamic_slice_in_dim(a[0], (1 - core) * half, half, 0)
    got = lax.ppermute(give, "row", [(0, 1), (1, 0), (2, 3)])
    buf_a = jnp.where(core == 0, jnp.stack([keep, got]), jnp.stack([got, keep]))
    buf_b = jnp.where(core == 0, keep, got)
    for dist in tree_stages(n_z):
        buf_a = tree_step(buf_a, 0, dist, row, n_z)
        buf_b = tree_step(buf_b, 1, dist, row, n_z)
    mine = jnp.concatenate([buf_a, buf_b[None]])
    other = lax.ppermute(mine, "row", [(i, i ^ 1) for i in range(n_row)])
    lo = jnp.where(core == 0, mine, other)
    hi = jnp.where(core == 0, other, mine)
    rows = jnp.concatenate([lo, hi], axis=1)
    d = cs[:, 0]
    swapped = lax.ppermute(d, "row", [(0, 1), (1, 0)])
    third = lax.ppermute(d, "row", [(2, 0)]) + lax.ppermute(d, "row", [(2, 1)])
    block = jnp.where(core == 0, jnp.stack([d, swapped, third]), jnp.stack([swapped, d, third]))
    for dist in tree_stages(n_z):
        block = tree_step(block, 0, dist, row, n_z)
    cols = gather_cols(cs, n_col).transpose(1, 2, 0, 3, 4).reshape(PIVOTS, rt, t, t)
    dd = gather_cols(block, n_col).transpose(1, 2, 0, 3, 4).reshape(PIVOTS, PIVOTS, t, t)

    eye = jnp.eye(t, dtype=jnp.float32)
    a = a.at[:, :, 0, :].set(jnp.where(col < PIVOTS, 0.0, a[:, :, 0, :]))
    a = a.at[0].set(jnp.where(row < PIVOTS, 0.0, a[0]))
    r = []
    c = []
    for p in range(PIVOTS):
        tile0 = jnp.where(col < PIVOTS, jnp.where(col == p, eye, 0.0), rows[p][:, 0])
        r.append(rows[p].at[:, 0].set(tile0))
        tile0 = jnp.where(row < PIVOTS, jnp.where(row == p, -eye, 0.0), cols[p][0])
        c.append(cols[p].at[0].set(tile0))
    dd = [[dd[p, q] for q in range(PIVOTS)] for p in range(PIVOTS)]
    for p in range(PIVOTS):
        inverse = newton_inverse(dd[p][p])
        r[p] = jnp.einsum("ij,jcl->icl", inverse, r[p], precision=HI)
        for q in range(p + 1, PIVOTS):
            dd[p][q] = jnp.dot(inverse, dd[p][q], precision=HI)
        for q in range(p + 1, PIVOTS):
            for s in range(p + 1, PIVOTS):
                dd[q][s] = dd[q][s] - jnp.dot(dd[q][p], dd[p][s], precision=HI)
            r[q] = r[q] - jnp.einsum("ij,jcl->icl", dd[q][p], r[p], precision=HI)
            c[q] = c[q] - jnp.einsum("aij,jl->ail", c[p], dd[p][q], precision=HI)
    cc = jnp.concatenate(c, axis=2)
    rr = jnp.concatenate(r, axis=0)
    a = a - jnp.einsum("aij,jcl->aicl", cc, rr, precision=HI)
    return a.reshape(matrix.shape)


def solution(mesh):
    spec = P(None, "row", None, None, "col", None)
    return jax.shard_map(local, mesh=mesh, in_specs=(spec,), out_specs=spec, check_vma=False)
```

```python
import jax
import jax.numpy as jnp
from jax import lax
from jax.experimental import pallas as pl
from jax.experimental.pallas import tpu as pltpu
from jax.sharding import PartitionSpec as P

PIVOTS = 3
HI = lax.Precision.HIGHEST
TREE = (
    ((0, 7),),
    ((0, 14), (7, 5)),
    ((7, 9), (5, 4), (0, 1), (14, 12)),
    ((7, 8), (9, 10), (4, 3), (5, 6), (1, 2), (0, 15), (14, 13), (12, 11)),
)


BLOCK_TREE = TREE[:3] + (
    ((0, 2), (1, 3), (4, 6), (5, 8), (7, 10), (9, 11), (12, 13), (14, 15)),
)


def permute(x, pairs):
    return lax.ppermute(x, "row", pairs)


def exchange(x):
    return lax.all_to_all(x, "col", 0, 0, tiled=True)


def tree_step(buf, hops, row):
    n_z = 16
    pairs = []
    for s, d in hops:
        pairs.append((2 * s, 2 * d))
        pairs.append((2 * (-s % n_z) + 1, 2 * (-d % n_z) + 1))
    recv = permute(buf, pairs)
    z = jnp.where(row % 2 == 0, row // 2, (n_z - row // 2) % n_z)
    hit = z == hops[0][1]
    for _, d in hops[1:]:
        hit = hit | (z == d)
    return jnp.where(hit, recv, buf)


def gather_cols(piece, n_col):
    return exchange(jnp.broadcast_to(piece[None], (n_col, *piece.shape)))


def mm(x, y):
    return jnp.dot(x, y, precision=HI, preferred_element_type=jnp.float32)


def split(x):
    hi = x.astype(jnp.bfloat16)
    return hi, (x - hi.astype(jnp.float32)).astype(jnp.bfloat16)


def mm_split(xh, xl, yh, yl):
    def one(p, q):
        return jnp.dot(p, q, preferred_element_type=jnp.float32)

    return one(xh, yh) + (one(xh, yl) + one(xl, yh))


def store_weights(row, gg, out):
    t = gg.shape[-1]
    ri = lax.broadcasted_iota(jnp.int32, (t, t), 0)
    ci = lax.broadcasted_iota(jnp.int32, (t, t), 1)
    same = ri == ci

    def newton(block):
        diag = jnp.where(same, block, 0.0)
        down = 1.0 / jnp.sum(diag, axis=1, keepdims=True)
        across = 1.0 / jnp.sum(diag, axis=0, keepdims=True)
        return jnp.where(same, 2.0 * down, 0.0) - down * block * across

    def lanes(*xs):
        return jnp.concatenate(xs, axis=1)

    rt = gg.shape[2] - PIVOTS
    d = [[gg[:, q, rt + p].reshape(t, t) for q in range(PIVOTS)] for p in range(PIVOTS)]
    inv0 = newton(d[0][0])
    l0 = mm(inv0, lanes(d[0][1], d[0][2]))
    p1 = mm(jnp.concatenate([d[1][0], d[2][0]]), lanes(l0, inv0))
    d11 = d[1][1] - p1[:t, :t]
    d21 = d[2][1] - p1[t:, :t]
    inv1 = newton(d11)
    l1 = mm(inv1, lanes(d[1][2] - p1[:t, t : 2 * t], -p1[:t, 2 * t :]))
    d12, t10 = l1[:, :t], l1[:, t:]
    t1 = lanes(t10, inv1)
    p2 = mm(d21, lanes(d12, t1))
    inv2 = newton(d[2][2] - p1[t:, t : 2 * t] - p2[:, :t])
    l2 = mm(inv2, lanes(-p1[t:, 2 * t :] - p2[:, t : 2 * t], -p2[:, 2 * t :]))
    w2 = lanes(l2, inv2)
    zero = jnp.zeros((t, t), jnp.float32)
    w1 = lanes(t1, zero) - mm(d12, w2)
    w12 = jnp.concatenate([w1, w2])
    w0 = lanes(inv0, zero, zero) - mm(l0, w12)
    wh, wl = split(jnp.concatenate([w0, w12]))
    for a in range(rt):
        c = lanes(*[gg[:, q, a].reshape(t, t) for q in range(PIVOTS)])
        if a == 0:
            wide_r = lax.broadcasted_iota(jnp.int32, c.shape, 0)
            wide_c = lax.broadcasted_iota(jnp.int32, c.shape, 1)
            unit = jnp.where(wide_c == row * t + wide_r, -1.0, 0.0)
            c = jnp.where(row < PIVOTS, unit, c)
        ch, cl = split(mm_split(*split(c), wh, wl))
        out[0, a * t : (a + 1) * t] = ch
        out[1, a * t : (a + 1) * t] = cl


def tail_kernel(idx, a_hbm, gg, mine, other, out_hbm, abuf, rbuf, cw, sem_a, sem_o):
    rows, ct, t = a_hbm.shape
    half = t // 2
    row, col = idx[0], idx[1]
    core = lax.rem(row, 2)
    lo = pl.multiple_of(core * half, half)
    hi = pl.multiple_of((1 - core) * half, half)
    tiles = [pl.ds(i * t, t) for i in range(rows // t)]
    loads = [
        pltpu.make_async_copy(a_hbm.at[s], abuf.at[s], sem_a.at[i]) for i, s in enumerate(tiles)
    ]
    for g in loads:
        g.start()
    store_weights(row, gg, cw)
    ch = cw[0]
    cl = cw[1]
    stores = []
    for b in range(0, ct, 2):
        for k in (b, b + 1):
            for p in range(PIVOTS):
                rbuf[k % 2, p, pl.ds(lo, half)] = mine[p, :, k]
                rbuf[k % 2, p, pl.ds(hi, half)] = other[p, :, k]
        if b == 0:

            @pl.when(col < PIVOTS)
            def _():
                ri = lax.broadcasted_iota(jnp.int32, (t, t), 0)
                ci = lax.broadcasted_iota(jnp.int32, (t, t), 1)
                eye = jnp.where(ri == ci, 1.0, 0.0)
                for p in range(PIVOTS):
                    rbuf[0, p] = jnp.where(col == p, eye, 0.0)

        r = jnp.concatenate(
            [rbuf[0].reshape(PIVOTS * t, t), rbuf[1].reshape(PIVOTS * t, t)], axis=1
        )
        prod = mm_split(ch, cl, *split(r))
        if b == 0:
            for g in loads:
                g.wait()

            @pl.when(row < PIVOTS)
            def _():
                abuf[:t] = jnp.zeros((t, ct, t), jnp.float32)

            @pl.when(col < PIVOTS)
            def _():
                abuf[:, 0] = jnp.zeros((rows, t), jnp.float32)

        last = b == ct - 2
        for i, s in enumerate(tiles):
            for k in (0, 1):
                part = prod[i * t : (i + 1) * t, k * t : (k + 1) * t]
                abuf[i * t : (i + 1) * t, b + k] = abuf[i * t : (i + 1) * t, b + k] - part
            if last:
                g = pltpu.make_async_copy(abuf.at[s], out_hbm.at[s], sem_o.at[i])
                g.start()
                stores.append(g)
    for g in stores:
        g.wait()


def local(matrix):
    n_row = lax.axis_size("row")
    n_col = lax.axis_size("col")
    row = lax.axis_index("row")
    col = lax.axis_index("col")
    core = row % 2
    rt, _, t, ct, _, _ = matrix.shape
    a = matrix.reshape(rt, t, ct, t)
    sub = t // n_col
    half = t // 2
    cp = a[:, :, 0, :].reshape(rt, n_col, sub, t).transpose(1, 0, 2, 3)
    cs = exchange(cp)[:PIVOTS]
    h0, h1 = a[0, :half], a[0, half:]
    keep = jnp.where(core == 0, h0, h1)
    give = jnp.where(core == 0, h1, h0)
    got = permute(give, [(0, 1), (1, 0)])
    p2 = jnp.where(core == 0, permute(h0, [(2, 0)]), permute(h1, [(2, 1)]))
    p0 = jnp.where(core == 0, keep, got)
    p1 = jnp.where(core == 0, got, keep)
    x = jnp.stack([p0, p1, p2])
    d = cs[:, 0]
    swapped = permute(d, [(0, 1), (1, 0)])
    third = permute(d, [(2, 0)]) + permute(d, [(2, 1)])
    block = jnp.where(
        core == 0, jnp.stack([d, swapped, third], 1), jnp.stack([swapped, d, third], 1)
    )
    for stage in range(len(TREE)):
        x = tree_step(x, TREE[stage], row)
        block = tree_step(block, BLOCK_TREE[stage], row)
    other = permute(x, [(i, i ^ 1) for i in range(n_row)])
    panels = gather_cols(jnp.concatenate([cs, block], axis=1), n_col)

    idx = jnp.stack([row, col]).astype(jnp.int32)
    smem = pl.BlockSpec(memory_space=pltpu.SMEM)
    vmem = pl.BlockSpec(memory_space=pltpu.VMEM)
    hbm = pl.BlockSpec(memory_space=pl.ANY)
    out = pl.pallas_call(
        tail_kernel,
        out_shape=jax.ShapeDtypeStruct((rt * t, ct, t), jnp.float32),
        in_specs=[smem, hbm, vmem, vmem, vmem],
        out_specs=hbm,
        scratch_shapes=[
            pltpu.VMEM((rt * t, ct, t), jnp.float32),
            pltpu.VMEM((2, PIVOTS, t, t), jnp.float32),
            pltpu.VMEM((2, rt * t, PIVOTS * t), jnp.bfloat16),
            pltpu.SemaphoreType.DMA((rt,)),
            pltpu.SemaphoreType.DMA((rt,)),
        ],
        name="tail",
        cost_estimate=pl.CostEstimate(
            flops=10**10, bytes_accessed=8 * 10**6, transcendentals=0
        ),
    )(idx, a.reshape(rt * t, ct, t), panels, x, other)
    return out.reshape(matrix.shape)


def solution(mesh):
    spec = P(None, "row", None, None, "col", None)
    return jax.shard_map(local, mesh=mesh, in_specs=(spec,), out_specs=spec, check_vma=False)
```
